512 devices in a mesh: leaf: 256 (over x, z, y), cols: 2 (over core).
Axes of the slice: x: 4, y: 4, z: 16, core: 2. Of those that a mesh axis runs over, the one named last changes fastest.
Arguments:
- vectors: bfloat16 [128, 524288], P('cols', 'leaf'), may hold values from -6 to 6
- near_blocks: bfloat16 [2048, 8, 256, 256], P('leaf', None, 'cols'), may hold values from -0.125 to 0.125
- near_index: int32 [2048, 8], P('leaf'), may hold values from -1 to 2047, as said below
- far_index: int32 [2048, 8], P('leaf'), may hold values from -1 to 2047, as said below
- far_kind: int32 [2048, 8], P('leaf'), may hold values from 0 to 15
- cluster_basis: bfloat16 [2048, 64, 256], P('leaf'), may hold values from -0.375 to 0.375
- leaf_transfer: float32 [2048, 64, 64], P('leaf'), may hold values from -0.25 to 0.25
- coupling_table: float32 [16, 64, 64], replicated, may hold values from -0.5 to 0.5
- parent_transfer_matrices: float32 [2, 64, 64], replicated, may hold values from -0.625 to 0.625
- coarse_kind: int32 [255], replicated, may hold values from 0 to 15
Outputs:
- product: bfloat16 [128, 524288], P('cols', 'leaf')
The draws below stay inside these ranges and needn't reach their ends.
Inputs may be any that keep to these rules, and one draw needn't show every extreme that they name: `near_index`: row i holds distinct leaves within 8 positions of leaf i, and -1 in unused slots; its first entry is i itself, its second is i - 8 for even i and i + 8 for odd i, or -1 where that is outside the leaves. No leaf stands in both near_index and far_index of one row. `far_index`: row i holds distinct leaves other than i within 8 positions of leaf i, and -1 in unused slots.
All inputs are finite; a program needn't handle non-finite values.
Results may differ from the reference program's by a relative error of at most 0.0044.
Values may be sent and summed in bfloat16 or wider, within the bound.
No kernel may reach another device: no remote copies, remote signals or barrier semaphores. Data moves between devices by JAX's collectives and lax.ppermute only.
A program may use at most 128 MiB of HBM per device.

```python
import jax
import jax.numpy as jnp
from jax import lax

LEAF = 256
RANK = 64
COLS = 128
LEAF_DEV = 8
K_NEAR = 8
K_FAR = 8
KINDS = 16
LEAVES = 2048
ROWS = 524288
GROUPS = 256
N_LEAF = 256


def window_lists(key):
    key_order = jax.random.fold_in(key, 71)
    key_near = jax.random.fold_in(key, 72)
    key_far = jax.random.fold_in(key, 73)
    candidates = jnp.concatenate([jnp.arange(-LEAF_DEV, 0, dtype=jnp.int32), jnp.arange(1, LEAF_DEV + 1, dtype=jnp.int32)])
    width_count = 2 * LEAF_DEV
    leaf_ids = jnp.arange(LEAVES, dtype=jnp.int32)[:, None]
    forced_offset = jnp.where(leaf_ids % 2 == 0, -LEAF_DEV, LEAF_DEV).astype(jnp.int32)
    is_forced = candidates[None, :] == forced_offset
    scores = jax.random.randint(key_order, (LEAVES, width_count), 0, 1 << 20, dtype=jnp.int32) * width_count + jnp.arange(width_count, dtype=jnp.int32)[None, :]
    scores = jnp.where(is_forced, (1 << 20) * width_count + width_count, scores)
    order = jnp.argsort(scores, axis=1)
    offsets = candidates[order]
    forced_target = leaf_ids + forced_offset
    forced_inside = (forced_target >= 0) & (forced_target < LEAVES)
    forced_entry = jnp.where(forced_inside, forced_target, -1)
    near_live = jax.random.randint(key_near, (LEAVES, 1), 0, K_NEAR - 1, dtype=jnp.int32)
    near_slots = jnp.arange(K_NEAR - 2, dtype=jnp.int32)[None, :] < near_live
    near_targets = leaf_ids + offsets[:, :K_NEAR - 2]
    near_inside = (near_targets >= 0) & (near_targets < LEAVES)
    near_list = jnp.concatenate([leaf_ids, forced_entry, jnp.where(near_slots & near_inside, near_targets, -1)], axis=1)
    far_live = jax.random.randint(key_far, (LEAVES, 1), 1, K_FAR + 1, dtype=jnp.int32)
    far_slots = jnp.arange(K_FAR, dtype=jnp.int32)[None, :] < far_live
    far_targets = leaf_ids + offsets[:, K_NEAR - 2:K_NEAR - 2 + K_FAR]
    far_inside = (far_targets >= 0) & (far_targets < LEAVES)
    far_list = jnp.where(far_slots & far_inside, far_targets, -1)
    return (near_list.astype(jnp.int32), far_list.astype(jnp.int32))


def draw_near_index(key, part):
    return window_lists(key)[0]


def draw_far_index(key, part):
    return window_lists(key)[1]


def touch_ends(drawn, key, smallest, largest):
    dims = drawn.shape
    place = [jax.random.randint(jax.random.fold_in(key, axis), (), 0, dims[axis]) for axis in range(len(dims))]
    drawn = drawn.at[tuple(place)].set(smallest)
    longest = dims.index(max(dims))
    place[longest] = (place[longest] + 1) % dims[longest]
    return drawn.at[tuple(place)].set(largest)


def levels(own_key, shape, pieces, low, high):
    factor_of, own = 1.0, jax.random.fold_in(own_key, 6)
    for axis_at, blocks in pieces:
        draws = jnp.exp(jax.random.uniform(jax.random.fold_in(own, axis_at), (blocks,), jnp.float32, low / len(pieces), high / len(pieces)))
        factor_of = factor_of * jnp.repeat(draws, shape[axis_at] // blocks).reshape([-1 if axis == axis_at else 1 for axis in range(len(shape))])
    return factor_of


def noise(own_key, extent, spread, bound, cuts=(), kind=jnp.bfloat16):
    result = jax.random.normal(own_key, extent, jnp.float32) * spread
    if len(cuts) > 0:
        result = levels(own_key, extent, cuts, -0.22, 0.18) * result
    return jnp.clip(result, min=-bound, max=bound).astype(kind)


def setup_inputs(seed: int = 0) -> dict:
    keys = jax.random.split(jax.random.key(seed), 11)
    vectors = noise(keys[0], (COLS, ROWS), 1.0, 6.0, ((0, 2), (1, 256)))
    near_blocks = noise(keys[1], (LEAVES, K_NEAR, LEAF, LEAF), (LEAF * K_NEAR) ** -0.5, 0.125, ((0, 256), (2, 2)))
    near_index = draw_near_index(jax.random.fold_in(keys[10], 71), 0)
    far_index = draw_far_index(jax.random.fold_in(keys[10], 71), 0)
    far_kind = touch_ends(jax.random.randint(keys[4], (LEAVES, K_FAR), 0, KINDS), jax.random.fold_in(keys[4], 1), 0, KINDS - 1).astype(jnp.int32)
    cluster_basis = noise(keys[5], (LEAVES, RANK, LEAF), LEAF ** -0.5, 0.375, ((0, 256),))
    leaf_transfer = noise(keys[6], (LEAVES, RANK, RANK), (LEAF_DEV * RANK) ** -0.5, 0.25, ((0, 256),), jnp.float32)
    coupling_table = noise(keys[7], (KINDS, RANK, RANK), (2 * RANK) ** -0.5, 0.5, (), jnp.float32)
    parent_transfer_matrices = noise(keys[8], (2, RANK, RANK), (RANK * 7 // 5) ** -0.5, 0.625, (), jnp.float32)
    coarse_kind = touch_ends(jax.random.randint(keys[9], (GROUPS - 1,), 0, KINDS), jax.random.fold_in(keys[9], 1), 0, KINDS - 1).astype(jnp.int32)
    return {"vectors": vectors, "near_blocks": near_blocks, "near_index": near_index, "far_index": far_index, "far_kind": far_kind, "cluster_basis": cluster_basis, "leaf_transfer": leaf_transfer, "coupling_table": coupling_table, "parent_transfer_matrices": parent_transfer_matrices, "coarse_kind": coarse_kind}


def coarse_tree(level_coefs, coarse_kind, coupling_table, parent_transfer_matrices):
    upper_level = lax.Precision.HIGHEST
    depth_count = level_coefs.shape[0].bit_length() - 1
    parent_chain = level_coefs
    couplings = []
    for depth_step in range(depth_count):
        node_count = parent_chain.shape[0]
        left_child_nodes = parent_chain[0::2]
        right_child_nodes = parent_chain[1::2]
        kind_rows = coarse_kind[node_count // 2 - 1:node_count - 1]
        lookup_tables = coupling_table[kind_rows]
        toward_left_child = jnp.einsum('jkw,jvw->jkv', right_child_nodes, lookup_tables, precision=upper_level)
        toward_right_child = jnp.einsum('ufo,uoz->ufz', left_child_nodes, lookup_tables, precision=upper_level)
        couplings.append(jnp.stack([toward_left_child, toward_right_child], axis=1).reshape(parent_chain.shape))
        if depth_step + 1 < depth_count:
            parent_chain = (jnp.einsum('mhw,vw->mhv', left_child_nodes, parent_transfer_matrices[0], precision=upper_level)
                         + jnp.einsum('mhw,vw->mhv', right_child_nodes, parent_transfer_matrices[1], precision=upper_level))
    descending_pass = couplings[-1]
    for depth_step in range(depth_count - 2, -1, -1):
        child_nodes = jnp.stack([jnp.einsum('fno,od->fnd', descending_pass, parent_transfer_matrices[0], precision=upper_level),
                              jnp.einsum('fno,od->fnd', descending_pass, parent_transfer_matrices[1], precision=upper_level)], axis=1)
        descending_pass = child_nodes.reshape(couplings[depth_step].shape) + couplings[depth_step]
    return descending_pass


def reference(vectors, near_blocks, near_index, far_index, far_kind, cluster_basis, leaf_transfer, coupling_table, parent_transfer_matrices, coarse_kind):
    upper_level = lax.Precision.HIGHEST
    leaf_count = cluster_basis.shape[0]
    basis_rank = cluster_basis.shape[1]
    leaf_rows = cluster_basis.shape[2]
    col_count = vectors.shape[0]
    vector_leaves = vectors.astype(jnp.float32).reshape(col_count, leaf_count, leaf_rows)
    basis_wide = cluster_basis.astype(jnp.float32)
    leaf_coefs = jnp.einsum('cir,iqr->icq', vector_leaves, basis_wide, precision=upper_level)
    grouped = leaf_coefs.reshape(N_LEAF, LEAF_DEV, col_count, basis_rank)
    transfers = leaf_transfer.reshape(N_LEAF, LEAF_DEV, basis_rank, basis_rank)
    group_coef = jnp.einsum('gics,girs->gcr', grouped, transfers, precision=upper_level)
    descending_pass = coarse_tree(group_coef, coarse_kind, coupling_table, parent_transfer_matrices)
    repeated = jnp.repeat(descending_pass, LEAF_DEV, axis=0)
    leaf_field = jnp.einsum('icr,irs->ics', repeated, leaf_transfer, precision=upper_level)
    far_sum = jnp.zeros_like(leaf_field)
    for slot_index in range(K_FAR):
        valid = far_index[:, slot_index] >= 0
        target = jnp.where(valid, far_index[:, slot_index], 0).astype(jnp.int32)
        picked = leaf_coefs[target] * valid[:, None, None].astype(jnp.float32)
        chosen = coupling_table[far_kind[:, slot_index]]
        far_sum = far_sum + jnp.einsum('ics,irs->icr', picked, chosen, precision=upper_level)
    leaf_field = leaf_field + far_sum
    field_rounded = lax.optimization_barrier(leaf_field.astype(jnp.bfloat16)).astype(jnp.float32)
    far_rows = jnp.einsum('ics,isq->ciq', field_rounded, basis_wide, precision=upper_level)
    near_sum = jnp.zeros_like(far_rows)
    for slot_index in range(K_NEAR):
        valid = near_index[:, slot_index] >= 0
        target = jnp.where(valid, near_index[:, slot_index], 0).astype(jnp.int32)
        picked_rows = vector_leaves[:, target, :] * valid[None, :, None].astype(jnp.float32)
        blocks = near_blocks[:, slot_index].astype(jnp.float32)
        near_sum = near_sum + jnp.einsum('cir,iqr->ciq', picked_rows, blocks, precision=upper_level)
    return (far_rows + near_sum).reshape(col_count, -1).astype(jnp.bfloat16)
```

```python
import jax
import jax.numpy as jnp
from jax import lax
from jax.experimental import pallas as pl
from jax.experimental.pallas import tpu as pltpu
from jax.sharding import PartitionSpec as P


F32 = jnp.float32
BF16 = jnp.bfloat16
NT = (((1,), (1,)), ((), ()))


def halves(value):
    high = value.astype(BF16)
    return high, (value - high.astype(F32)).astype(BF16)


def triple_left(value):
    high, low = halves(value)
    return jnp.concatenate([high, low, high], axis=1)


def triple_right(value):
    high, low = halves(value)
    return jnp.concatenate([high, high, low], axis=0)


def dot(left, right):
    return jnp.dot(left, right, preferred_element_type=F32)


def dot_nt(left, right):
    return lax.dot_general(left, right, NT, preferred_element_type=F32)


def fold(value, rank):
    return value[:, :rank] + value[:, rank : 2 * rank]


def lanes(value):
    part = value.shape[0] // 2
    return jnp.concatenate([value[:part], value[part:]], axis=1)


def unlanes(value):
    rank = value.shape[1] // 2
    return jnp.concatenate([value[:, :rank], value[:, rank:]], axis=0)


def bring(sources, targets, arrived):
    copies = [
        pltpu.make_async_copy(source, target, arrived.at[n])
        for n, (source, target) in enumerate(zip(sources, targets))
    ]
    for copy in copies:
        copy.start()
    return copies


def coef_kernel(
    x_hbm, basis_hbm, transfer_hbm, packed_ref, group_ref, x_ref, basis_ref, transfer_ref, arrived
):
    leaves, rank, rows = basis_ref.shape
    for copy in bring(
        (x_hbm, basis_hbm, transfer_hbm), (x_ref, basis_ref, transfer_ref), arrived
    ):
        copy.wait()
    total = jnp.zeros((x_ref.shape[0], rank), F32)
    for i in range(leaves):
        coef = dot_nt(x_ref[:, i * rows : (i + 1) * rows], basis_ref[i])
        start = leaves * rows + i * 2 * rank
        high, low = halves(coef)
        both = jnp.concatenate([high, low], axis=1)
        packed_ref[:, start : start + 2 * rank] = both
        above, below = halves(transfer_ref[i])
        total += dot_nt(both, jnp.concatenate([above, above], axis=1)) + dot_nt(high, below)
    sent = lanes(total.astype(BF16))
    for j in range(group_ref.shape[0]):
        group_ref[j] = sent
    packed_ref[:, : leaves * rows] = x_ref[...]


def path_blocks(g, groups, first, last, down, kind_ref, table_ref, parent_ref, with_sum):
    rank = table_ref.shape[1]
    steps = [triple_left(parent_ref[0]), triple_left(parent_ref[1])]
    across = []
    for level in range(first, last):
        heap = (groups >> (level + 1)) + (g >> (level + 1))
        coupling = table_ref[kind_ref[heap - 1]]
        bit = (g >> level) & 1
        coupling = jnp.where(bit == 1, coupling, coupling.T)
        step = jnp.where(bit == 1, parent_ref[1], parent_ref[0])
        if down is None:
            across.append(coupling)
            down = step
        else:
            right = triple_right(down)
            made = dot(triple_left(jnp.concatenate([coupling, step], axis=0)), right)
            across.append(made[:rank])
            down = made[rank:]
    upward = jnp.concatenate([parent_ref[0].T, parent_ref[1].T], axis=0)
    left = triple_left(upward)
    trees = [[block] for block in across]
    if with_sum:
        trees.append([upward[:rank], upward[rank:]])
    for step in range(1, last - first):
        live = [t for t in range(len(trees)) if t >= step]
        blocks = [block for t in live for block in trees[t]]
        made = dot(left, triple_right(jnp.concatenate(blocks, axis=1)))
        at = 0
        for t in live:
            grown = []
            for _ in trees[t]:
                for b in range(2):
                    grown.append(made[b * rank : (b + 1) * rank, at * rank : (at + 1) * rank])
                at += 1
            trees[t] = grown
    return trees, down


def store_blocks(trees, here, ref):
    rank = ref.shape[1]
    ref[here] = jnp.zeros((rank, ref.shape[2]), BF16)
    for t, blocks in enumerate(trees):
        base = ((here >> t) ^ 1) << t
        for v, block in enumerate(blocks):
            ref[base + v, :, : 2 * rank] = jnp.concatenate(halves(block), axis=1)


def low_path_kernel(
    kind_hbm, table_hbm, parent_hbm, low_ref, down_ref, kind_ref, table_ref, parent_ref, arrived
):
    for copy in bring(
        (kind_hbm, table_hbm, parent_hbm), (kind_ref, table_ref, parent_ref), arrived
    ):
        copy.wait()
    g = lax.axis_index("leaf")
    groups = kind_ref.shape[0] + 1
    half = (groups.bit_length() - 1) // 2
    rank = table_ref.shape[1]
    trees, down = path_blocks(
        g, groups, 0, half, None, kind_ref, table_ref, parent_ref, True
    )
    down_ref[...] = down
    store_blocks(trees[:half], g & ((1 << half) - 1), low_ref)
    for j, block in enumerate(trees[half]):
        low_ref[j, :, 2 * rank :] = jnp.concatenate(halves(block), axis=1)


def high_path_kernel(
    kind_hbm, table_hbm, parent_hbm, transfer_hbm, down_ref, high_ref, far_ref, spread_ref,
    kind_ref, table_ref, parent_ref, transfer_ref, arrived,
):
    for copy in bring(
        (kind_hbm, table_hbm, parent_hbm, transfer_hbm),
        (kind_ref, table_ref, parent_ref, transfer_ref),
        arrived,
    ):
        copy.wait()
    g = lax.axis_index("leaf")
    groups = kind_ref.shape[0] + 1
    depth = groups.bit_length() - 1
    half = depth // 2
    rank = table_ref.shape[1]
    for kind in range(table_ref.shape[0]):
        high, low = halves(table_ref[kind])
        far_ref[kind, :rank, :] = jnp.concatenate([high, high], axis=1)
        far_ref[kind, rank:, :] = jnp.concatenate([low, jnp.zeros_like(low)], axis=1)
    for i in range(transfer_ref.shape[0]):
        spread_ref[i] = triple_right(transfer_ref[i])
    trees, _ = path_blocks(
        g, groups, half, depth, down_ref[...], kind_ref, table_ref, parent_ref, False
    )
    store_blocks(trees, g >> half, high_ref)


def middle_kernel(seen_ref, low_ref, own_ref, sent_ref):
    count = seen_ref.shape[0]
    rank = low_ref.shape[1]
    total = dot(unlanes(seen_ref[0]), low_ref[0])
    for j in range(1, count):
        total += dot(unlanes(seen_ref[j]), low_ref[j])
    own_ref[...] = fold(total[:, : 2 * rank], rank)
    sent = lanes(fold(total[:, 2 * rank :], rank).astype(BF16))
    for j in range(count):
        sent_ref[j] = sent


def near_kernel(
    near_hbm, far_index_hbm, far_kind_hbm,
    before_ref, packed_ref, after_ref, own_ref, other_ref, table_ref,
    near_out_ref, far_out_ref, window, coefs, blocks, arrived,
    near_ref, far_index_ref, far_kind_ref, lists_arrived,
):
    lists = bring(
        (near_hbm, far_index_hbm, far_kind_hbm), (near_ref, far_index_ref, far_kind_ref),
        lists_arrived,
    )
    leaves, slots, half, rows = own_ref.shape
    cols = packed_ref.shape[0]
    rank = far_out_ref.shape[2]
    start = (lax.axis_index("leaf") - 1) * leaves
    core = lax.axis_index("cols")

    def fetch(i, side):
        ref = (own_ref, other_ref)[side]
        row = (core if side == 0 else 1 - core) * half
        to = blocks.at[i, :, pl.ds(pl.multiple_of(row, half), half), :]
        return pltpu.make_async_copy(ref.at[i], to, arrived.at[side, i])

    for i in range(leaves):
        for side in range(2):
            fetch(i, side).start()
    for part, ref in enumerate((before_ref, packed_ref, after_ref)):
        for n in range(leaves):
            window[part * leaves + n] = ref[:, n * rows : (n + 1) * rows]
            at = leaves * rows + n * 2 * rank
            coefs[part * leaves + n] = ref[:, at : at + 2 * rank]
    window[3 * leaves] = jnp.zeros((cols, rows), BF16)
    coefs[3 * leaves] = jnp.zeros((cols, 2 * rank), BF16)
    for copy in lists:
        copy.wait()

    def slot(index):
        return jnp.where(index >= 0, jnp.clip(index - start, 0, 3 * leaves - 1), 3 * leaves)

    def far_leaf(i, carry):
        total = jnp.zeros((cols, 2 * rank), F32)
        for k in range(slots):
            total += dot_nt(coefs[slot(far_index_ref[i, k])], table_ref[far_kind_ref[i, k]])
        far_out_ref[i] = fold(total, rank)
        return carry

    def near_leaf(i, carry):
        for side in range(2):
            fetch(i, side).wait()
        total = jnp.zeros((cols, rows), F32)
        for k in range(slots):
            total += dot_nt(window[slot(near_ref[i, k])], blocks[i, k])
        near_out_ref[:, pl.ds(pl.multiple_of(i * rows, rows), rows)] = total
        return carry

    lax.fori_loop(0, leaves, far_leaf, 0)
    lax.fori_loop(0, leaves, near_leaf, 0)


def last_kernel(seen_ref, high_ref, own_ref, spread_ref, far_ref, near_ref, basis_ref, out_ref):
    count = seen_ref.shape[0]
    leaves, rank, rows = basis_ref.shape
    total = dot(unlanes(seen_ref[0]), high_ref[0])
    for j in range(1, count):
        total += dot(unlanes(seen_ref[j]), high_ref[j])
    group = triple_left(own_ref[...] + fold(total, rank))
    for i in range(leaves):
        field = (dot(group, spread_ref[i]) + far_ref[i]).astype(BF16)
        at = slice(i * rows, (i + 1) * rows)
        out_ref[:, at] = (near_ref[:, at] + dot(field, basis_ref[i])).astype(BF16)


def call(kernel, outs, ins, flops, moved, mib, scratch=()):
    def spec(space):
        return pl.BlockSpec(memory_space=space)

    many = isinstance(outs, tuple)
    return pl.pallas_call(
        kernel,
        out_shape=outs,
        in_specs=[spec(space) for space in ins],
        out_specs=tuple(spec(pltpu.VMEM) for _ in outs) if many else spec(pltpu.VMEM),
        scratch_shapes=list(scratch),
        compiler_params=pltpu.CompilerParams(vmem_limit_bytes=mib << 20),
        cost_estimate=pl.CostEstimate(flops=flops, bytes_accessed=moved, transcendentals=0),
    )


def shards(
    vectors, near_blocks, near_index, far_index, far_kind,
    cluster_basis, leaf_transfer, coupling_table, parent_transfer_matrices, coarse_kind,
):
    cols, width = vectors.shape
    leaves, rank, rows = cluster_basis.shape
    slots = near_index.shape[1]
    kinds = coupling_table.shape[0]
    peers = lax.axis_size("leaf")
    half = (peers.bit_length() - 1) // 2
    size = 1 << half
    shape = jax.ShapeDtypeStruct
    packed_width = width + leaves * 2 * rank
    vm, hbm = pltpu.VMEM, pltpu.HBM
    kept = lambda space, array: space(array.shape, array.dtype)
    sems = lambda *count: pltpu.SemaphoreType.DMA(count)
    message = shape((size, cols // 2, 2 * rank), BF16)
    low_groups = [[n * size + j for j in range(size)] for n in range(size)]
    high_groups = [[n * size + j for n in range(size)] for j in range(size)]
    up = [(n, n + 1) for n in range(peers - 1)]
    stay = lambda *arrays: [pltpu.with_memory_space_constraint(a, hbm) for a in arrays]
    (
        vectors, blocks_here, near_index, far_index, far_kind, basis_here, transfer_here,
        coupling_table, parent_transfer_matrices, coarse_kind,
    ) = stay(
        vectors, near_blocks, near_index, far_index, far_kind, cluster_basis, leaf_transfer,
        coupling_table, parent_transfer_matrices, coarse_kind,
    )

    packed, group = call(
        coef_kernel, (shape((cols, packed_width), BF16), message),
        [hbm] * 3, 2**26, 2**20, 4,
        [kept(vm, vectors), kept(vm, cluster_basis), kept(vm, leaf_transfer), sems(3)],
    )(vectors, basis_here, transfer_here)
    seen_low = lax.all_to_all(
        group, "leaf", 0, 0, axis_index_groups=low_groups, tiled=True
    )
    before = lax.ppermute(packed, "leaf", up)
    after = lax.ppermute(packed, "leaf", [(b, a) for a, b in up])
    other_blocks = lax.ppermute(near_blocks, "cols", [(0, 1), (1, 0)])
    low_table, down = call(
        low_path_kernel,
        (shape((size, rank, 4 * rank), BF16), shape((rank, rank), F32)),
        [hbm] * 3, 2**27, 2**20, 6,
        [
            kept(pltpu.SMEM, coarse_kind), kept(vm, coupling_table),
            kept(vm, parent_transfer_matrices), sems(3),
        ],
    )(coarse_kind, coupling_table, parent_transfer_matrices)
    own, sent = call(
        middle_kernel, (shape((cols, rank), F32), message),
        [vm] * 2, 2**25, 2**19, 4,
    )(seen_low, low_table)
    seen_high = lax.all_to_all(sent, "leaf", 0, 0, axis_index_groups=high_groups, tiled=True)
    high_table, far_table, spread = call(
        high_path_kernel,
        (
            shape((size, rank, 2 * rank), BF16),
            shape((kinds, 2 * rank, 2 * rank), BF16),
            shape((leaves, 3 * rank, rank), BF16),
        ),
        [hbm] * 4 + [vm], 2**27, 2**20, 8,
        [
            kept(pltpu.SMEM, coarse_kind), kept(vm, coupling_table),
            kept(vm, parent_transfer_matrices), kept(vm, leaf_transfer), sems(4),
        ],
    )(coarse_kind, coupling_table, parent_transfer_matrices, transfer_here, down)
    near, far = call(
        near_kernel,
        (shape((cols, width), F32), shape((leaves, cols, rank), F32)),
        [hbm] * 3 + [vm] * 3 + [hbm] * 2 + [vm], 2**30, 10 * 2**20, 16,
        [
            pltpu.VMEM((3 * leaves + 1, cols, rows), BF16),
            pltpu.VMEM((3 * leaves + 1, cols, 2 * rank), BF16),
            pltpu.VMEM((leaves, slots, rows, rows), BF16),
            sems(2, leaves),
            kept(pltpu.SMEM, near_index), kept(pltpu.SMEM, far_index),
            kept(pltpu.SMEM, far_kind), sems(3),
        ],
    )(
        near_index, far_index, far_kind,
        before, packed, after, blocks_here, stay(other_blocks)[0], far_table,
    )
    return call(
        last_kernel, shape((cols, width), BF16), [vm] * 7, 2**27, 2**21, 8
    )(seen_high, high_table, own, spread, far, near, cluster_basis)


def solution(mesh):
    in_specs = (
        P("cols", "leaf"),
        P("leaf", None, "cols", None),
        P("leaf", None),
        P("leaf", None),
        P("leaf", None),
        P("leaf", None, None),
        P("leaf", None, None),
        P(),
        P(),
        P(),
    )
    out_specs = P("cols", "leaf")
    return jax.shard_map(shards, mesh=mesh, in_specs=in_specs, out_specs=out_specs, check_vma=False)
```

```python
import jax
import jax.numpy as jnp
from jax import lax
from jax.experimental import pallas as pl
from jax.experimental.pallas import tpu as pltpu
from jax.sharding import PartitionSpec as P


F32 = jnp.float32
BF16 = jnp.bfloat16
Y_BITS, Z_BITS, X_BITS = 2, 4, 2
NT = (((1,), (1,)), ((), ()))


def halves(value):
    high = value.astype(BF16)
    return high, (value - high.astype(F32)).astype(BF16)


def triple_left(value):
    high, low = halves(value)
    return jnp.concatenate([high, low, high], axis=1)


def triple_right(value):
    high, low = halves(value)
    return jnp.concatenate([high, high, low], axis=0)


def dot(left, right):
    return jnp.dot(left, right, preferred_element_type=F32)


def dot_nt(left, right):
    return lax.dot_general(left, right, NT, preferred_element_type=F32)


def fold(value, rank):
    return value[:, :rank] + value[:, rank : 2 * rank]


def lanes(value):
    part = value.shape[0] // 2
    return jnp.concatenate([value[:part], value[part:]], axis=1)


def unlanes(value):
    rank = value.shape[1] // 2
    return jnp.concatenate([value[:, :rank], value[:, rank:]], axis=0)


def bring(sources, targets, arrived):
    copies = [
        pltpu.make_async_copy(source, target, arrived.at[n])
        for n, (source, target) in enumerate(zip(sources, targets))
    ]
    for copy in copies:
        copy.start()
    return copies


def coef_kernel(
    x_hbm, basis_hbm, transfer_hbm, parent_hbm, packed_ref, group_ref, own_ref,
    x_ref, basis_ref, transfer_ref, parent_ref, arrived,
):
    leaves, rank, rows = basis_ref.shape
    copies = bring(
        (parent_hbm, x_hbm, basis_hbm, transfer_hbm),
        (parent_ref, x_ref, basis_ref, transfer_ref),
        arrived,
    )
    g = lax.axis_index("leaf")
    copies[0].wait()
    rise = None
    for level in range(Y_BITS):
        step = jnp.where(((g >> level) & 1) == 1, parent_ref[1], parent_ref[0])
        rise = step if rise is None else dot(triple_left(step), triple_right(rise))
    rise = triple_right(rise.T)
    for copy in copies[1:3]:
        copy.wait()
    packed_ref[:, : leaves * rows] = x_ref[...]
    pairs = []
    for i in range(leaves):
        high, low = halves(dot_nt(x_ref[:, i * rows : (i + 1) * rows], basis_ref[i]))
        both = jnp.concatenate([high, low], axis=1)
        start = leaves * rows + i * 2 * rank
        packed_ref[:, start : start + 2 * rank] = both
        pairs.append((high, both))
    copies[3].wait()
    total = jnp.zeros((x_ref.shape[0], rank), F32)
    for i, (high, both) in enumerate(pairs):
        above, below = halves(transfer_ref[i])
        total += dot_nt(both, jnp.concatenate([above, above], axis=1)) + dot_nt(high, below)
    sent = lanes(dot(triple_left(total), rise).astype(BF16))
    for j in range(group_ref.shape[0]):
        group_ref[j] = sent
    own_ref[...] = lanes(total.astype(BF16))


def path_blocks(g, groups, first, last, down, kind_ref, table_ref, parent_ref, with_sum):
    rank = table_ref.shape[1]
    steps = [triple_left(parent_ref[0]), triple_left(parent_ref[1])]
    across = []
    for level in range(first, last):
        heap = (groups >> (level + 1)) + (g >> (level + 1))
        coupling = table_ref[kind_ref[heap - 1]]
        bit = (g >> level) & 1
        coupling = jnp.where(bit == 1, coupling, coupling.T)
        step = jnp.where(bit == 1, parent_ref[1], parent_ref[0])
        if down is None:
            across.append(coupling)
            down = step
        else:
            right = triple_right(down)
            made = dot(triple_left(jnp.concatenate([coupling, step], axis=0)), right)
            across.append(made[:rank])
            down = made[rank:]
    upward = jnp.concatenate([parent_ref[0].T, parent_ref[1].T], axis=0)
    left = triple_left(upward)
    trees = [[block] for block in across]
    if with_sum:
        trees.append([upward[:rank], upward[rank:]])
    for step in range(1, last - first):
        live = [t for t in range(len(trees)) if t >= step]
        blocks = [block for t in live for block in trees[t]]
        made = dot(left, triple_right(jnp.concatenate(blocks, axis=1)))
        at = 0
        for t in live:
            grown = []
            for _ in trees[t]:
                for b in range(2):
                    grown.append(made[b * rank : (b + 1) * rank, at * rank : (at + 1) * rank])
                at += 1
            trees[t] = grown
    return trees, down


def store_blocks(trees, here, ref, offset):
    rank = ref.shape[1]
    ref[offset + here, :, : 2 * rank] = jnp.zeros((rank, 2 * rank), BF16)
    for t, blocks in enumerate(trees):
        base = ((here >> t) ^ 1) << t
        for v, block in enumerate(blocks):
            ref[offset + base + v, :, : 2 * rank] = jnp.concatenate(halves(block), axis=1)


def path_kernel(
    kind_hbm, table_hbm, parent_hbm, transfer_hbm, z_ref, yx_ref, fall_ref, far_ref, spread_ref,
    kind_ref, table_ref, parent_ref, transfer_ref, arrived,
):
    for copy in bring(
        (kind_hbm, table_hbm, parent_hbm, transfer_hbm),
        (kind_ref, table_ref, parent_ref, transfer_ref),
        arrived,
    ):
        copy.wait()
    g = lax.axis_index("leaf")
    groups = kind_ref.shape[0] + 1
    rank = table_ref.shape[1]
    low, high = Y_BITS, Y_BITS + Z_BITS
    tree = (kind_ref, table_ref, parent_ref)

    trees, inner = path_blocks(g, groups, low, high, None, *tree, True)
    store_blocks(trees[:Z_BITS], (g >> low) & ((1 << Z_BITS) - 1), z_ref, 0)
    for j, block in enumerate(trees[Z_BITS]):
        z_ref[j, :, 2 * rank :] = jnp.concatenate(halves(block), axis=1)

    y_trees, fall = path_blocks(g, groups, 0, low, None, *tree, False)
    fall_ref[...] = jnp.concatenate(halves(fall), axis=1)
    down = dot(triple_left(inner), triple_right(fall))
    x_trees, _ = path_blocks(g, groups, high, high + X_BITS, down, *tree, False)
    here = g >> high
    for t, blocks in enumerate(x_trees):
        base = ((here >> t) ^ 1) << t
        for v, block in enumerate(blocks):
            both = jnp.concatenate(halves(block), axis=1)
            for y in range(1 << Y_BITS):
                yx_ref[((base + v) << Y_BITS) + y] = both
    store_blocks(y_trees, g & ((1 << Y_BITS) - 1), yx_ref, here << Y_BITS)

    for kind in range(table_ref.shape[0]):
        above, below = halves(table_ref[kind])
        far_ref[kind, :rank, :] = jnp.concatenate([above, above], axis=1)
        far_ref[kind, rank:, :] = jnp.concatenate([below, jnp.zeros_like(below)], axis=1)
    for i in range(transfer_ref.shape[0]):
        spread_ref[i] = triple_right(transfer_ref[i])


def middle_kernel(seen_ref, z_ref, own_ref, sent_ref):
    count = seen_ref.shape[0]
    rank = z_ref.shape[1]
    rows = own_ref.shape[0]
    total = dot(unlanes(seen_ref[0]), z_ref[0])
    for j in range(1, count):
        total += dot(unlanes(seen_ref[j]), z_ref[j])
    inside = lanes(fold(total[:, : 2 * rank], rank).astype(BF16))
    outside = lanes(fold(total[:, 2 * rank :], rank).astype(BF16))
    own = own_ref[...]
    here = lax.axis_index("leaf") >> (Y_BITS + Z_BITS)
    for x in range(1 << X_BITS):
        mine = here == x
        first, second = jnp.where(mine, own, outside), jnp.where(mine, inside, outside)
        for y in range(1 << Y_BITS):
            sent_ref[(x << Y_BITS) + y, :rows] = first
            sent_ref[(x << Y_BITS) + y, rows:] = second


def near_kernel(
    near_hbm, far_index_hbm, far_kind_hbm,
    before_ref, packed_ref, after_ref, own_ref, other_ref, table_ref,
    out_ref, window, coefs, blocks, arrived,
    near_ref, far_index_ref, far_kind_ref, lists_arrived,
):
    lists = bring(
        (near_hbm, far_index_hbm, far_kind_hbm), (near_ref, far_index_ref, far_kind_ref),
        lists_arrived,
    )
    leaves, slots, half, rows = own_ref.shape
    cols = packed_ref.shape[0]
    rank = coefs.shape[2] // 2
    start = (lax.axis_index("leaf") - 1) * leaves
    core = lax.axis_index("cols")

    def fetch(i, side):
        ref = (own_ref, other_ref)[side]
        row = (core if side == 0 else 1 - core) * half
        to = blocks.at[i, :, pl.ds(pl.multiple_of(row, half), half), :]
        return pltpu.make_async_copy(ref.at[i], to, arrived.at[side, i])

    for i in range(leaves):
        for side in range(2):
            fetch(i, side).start()
    for part, ref in enumerate((before_ref, packed_ref, after_ref)):
        for n in range(leaves):
            window[part * leaves + n] = ref[:, n * rows : (n + 1) * rows]
            at = leaves * rows + n * 2 * rank
            coefs[part * leaves + n] = ref[:, at : at + 2 * rank]
    window[3 * leaves] = jnp.zeros((cols, rows), BF16)
    coefs[3 * leaves] = jnp.zeros((cols, 2 * rank), BF16)
    for copy in lists:
        copy.wait()

    def slot(index):
        return jnp.where(index >= 0, jnp.clip(index - start, 0, 3 * leaves - 1), 3 * leaves)

    def far_leaf(i):
        total = jnp.zeros((cols, 2 * rank), F32)
        for k in range(slots):
            total += dot_nt(coefs[slot(far_index_ref[i, k])], table_ref[far_kind_ref[i, k]])
        return fold(total, rank)

    for i in range(0, leaves, 2):
        at = leaves * rows + i * rank
        out_ref[:, at : at + 2 * rank] = jnp.concatenate([far_leaf(i), far_leaf(i + 1)], axis=1)
    for i in range(leaves):
        if i % 2 == 0:
            for n in (i, i + 1):
                for side in range(2):
                    fetch(n, side).wait()
        total = jnp.zeros((cols, rows), F32)
        for k in range(slots):
            total += dot_nt(window[slot(near_ref[i, k])], blocks[i, k])
        out_ref[:, i * rows : (i + 1) * rows] = total


def last_kernel(seen_ref, yx_ref, fall_ref, spread_ref, local_ref, basis_ref, out_ref):
    count, rows, _ = seen_ref.shape
    leaves, rank, width = basis_ref.shape
    half = rows // 2
    start = (lax.axis_index("leaf") >> (Y_BITS + Z_BITS)) << Y_BITS
    total = dot(unlanes(seen_ref[0, :half]), yx_ref[0])
    for j in range(1, count):
        total += dot(unlanes(seen_ref[j, :half]), yx_ref[j])
    for y in range(1 << Y_BITS):
        total += dot(unlanes(seen_ref[start + y, half:]), fall_ref[...])
    group = triple_left(fold(total, rank))
    for i in range(leaves):
        far = local_ref[:, leaves * width + i * rank : leaves * width + (i + 1) * rank]
        field = (dot(group, spread_ref[i]) + far).astype(BF16)
        at = slice(i * width, (i + 1) * width)
        out_ref[:, at] = (local_ref[:, at] + dot(field, basis_ref[i])).astype(BF16)


def call(kernel, outs, ins, flops, moved, mib, scratch=()):
    def spec(space):
        return pl.BlockSpec(memory_space=space)

    many = isinstance(outs, tuple)
    return pl.pallas_call(
        kernel,
        out_shape=outs,
        in_specs=[spec(space) for space in ins],
        out_specs=tuple(spec(pltpu.VMEM) for _ in outs) if many else spec(pltpu.VMEM),
        scratch_shapes=list(scratch),
        compiler_params=pltpu.CompilerParams(vmem_limit_bytes=mib << 20),
        cost_estimate=pl.CostEstimate(flops=flops, bytes_accessed=moved, transcendentals=0),
    )


def shards(
    vectors, near_blocks, near_index, far_index, far_kind,
    cluster_basis, leaf_transfer, coupling_table, parent_transfer_matrices, coarse_kind,
):
    cols, width = vectors.shape
    leaves, rank, rows = cluster_basis.shape
    slots = near_index.shape[1]
    kinds = coupling_table.shape[0]
    peers = lax.axis_size("leaf")
    size = 1 << Z_BITS
    across = 1 << (X_BITS + Y_BITS)
    shape = jax.ShapeDtypeStruct
    packed_width = width + leaves * 2 * rank
    vm, hbm = pltpu.VMEM, pltpu.HBM
    kept = lambda space, array: space(array.shape, array.dtype)
    sems = lambda *count: pltpu.SemaphoreType.DMA(count)
    own_line = shape((cols // 2, 2 * rank), BF16)
    line = (1 << Z_BITS) - 1
    z_groups, yx_groups = {}, {}
    for n in range(peers):
        z_groups.setdefault(n & ~(line << Y_BITS), []).append(n)
        yx_groups.setdefault((n >> Y_BITS) & line, []).append(n)
    z_groups, yx_groups = list(z_groups.values()), list(yx_groups.values())
    up = [(n, n + 1) for n in range(peers - 1)]
    stay = lambda *arrays: [pltpu.with_memory_space_constraint(a, hbm) for a in arrays]
    (
        vectors, blocks_here, near_index, far_index, far_kind, basis_here, transfer_here,
        coupling_table, parent_transfer_matrices, coarse_kind,
    ) = stay(
        vectors, near_blocks, near_index, far_index, far_kind, cluster_basis, leaf_transfer,
        coupling_table, parent_transfer_matrices, coarse_kind,
    )

    packed, group, own = call(
        coef_kernel,
        (
            shape((cols, packed_width), BF16),
            shape((size, *own_line.shape), BF16),
            own_line,
        ),
        [hbm] * 4, 2**26, 2**20, 4,
        [
            kept(vm, vectors), kept(vm, cluster_basis), kept(vm, leaf_transfer),
            kept(vm, parent_transfer_matrices), sems(4),
        ],
    )(vectors, basis_here, transfer_here, parent_transfer_matrices)
    seen_z = lax.all_to_all(group, "leaf", 0, 0, axis_index_groups=z_groups, tiled=True)
    before = lax.ppermute(packed, "leaf", up)
    after = lax.ppermute(packed, "leaf", [(b, a) for a, b in up])
    other_blocks = lax.ppermute(near_blocks, "cols", [(0, 1), (1, 0)])
    z_table, yx_table, fall, far_table, spread = call(
        path_kernel,
        (
            shape((size, rank, 4 * rank), BF16),
            shape((across, rank, 2 * rank), BF16),
            shape((rank, 2 * rank), BF16),
            shape((kinds, 2 * rank, 2 * rank), BF16),
            shape((leaves, 3 * rank, rank), BF16),
        ),
        [hbm] * 4, 2**28, 2**20, 8,
        [
            kept(pltpu.SMEM, coarse_kind), kept(vm, coupling_table),
            kept(vm, parent_transfer_matrices), kept(vm, leaf_transfer), sems(4),
        ],
    )(coarse_kind, coupling_table, parent_transfer_matrices, transfer_here)
    sent = call(
        middle_kernel, shape((across, cols, 2 * rank), BF16),
        [vm] * 3, 2**25, 2**19, 4,
    )(seen_z, z_table, own)
    seen_yx = lax.all_to_all(sent, "leaf", 0, 0, axis_index_groups=yx_groups, tiled=True)
    local = call(
        near_kernel,
        shape((cols, width + leaves * rank), F32),
        [hbm] * 3 + [vm] * 3 + [hbm] * 2 + [vm], 2**30, 10 * 2**20, 16,
        [
            pltpu.VMEM((3 * leaves + 1, cols, rows), BF16),
            pltpu.VMEM((3 * leaves + 1, cols, 2 * rank), BF16),
            pltpu.VMEM((leaves, slots, rows, rows), BF16),
            sems(2, leaves),
            kept(pltpu.SMEM, near_index), kept(pltpu.SMEM, far_index),
            kept(pltpu.SMEM, far_kind), sems(3),
        ],
    )(
        near_index, far_index, far_kind,
        before, packed, after, blocks_here, stay(other_blocks)[0], far_table,
    )
    return call(
        last_kernel, shape((cols, width), BF16), [vm] * 6, 2**27, 2**21, 8
    )(seen_yx, yx_table, fall, spread, local, cluster_basis)


def solution(mesh):
    in_specs = (
        P("cols", "leaf"),
        P("leaf", None, "cols", None),
        P("leaf", None),
        P("leaf", None),
        P("leaf", None),
        P("leaf", None, None),
        P("leaf", None, None),
        P(),
        P(),
        P(),
    )
    out_specs = P("cols", "leaf")
    return jax.shard_map(shards, mesh=mesh, in_specs=in_specs, out_specs=out_specs, check_vma=False)
```

```python
import jax
import jax.numpy as jnp
from jax import lax
from jax.experimental import pallas as pl
from jax.experimental.pallas import tpu as pltpu
from jax.sharding import PartitionSpec as P


F32 = jnp.float32
BF16 = jnp.bfloat16
Y_BITS, Z_BITS, X_BITS = 2, 4, 2
NT = (((1,), (1,)), ((), ()))


def halves(value):
    high = value.astype(BF16)
    return high, (value - high.astype(F32)).astype(BF16)


def triple_left(value):
    high, low = halves(value)
    return jnp.concatenate([high, low, high], axis=1)


def triple_right(value):
    high, low = halves(value)
    return jnp.concatenate([high, high, low], axis=0)


def dot(left, right):
    return jnp.dot(left, right, preferred_element_type=F32)


def dot_nt(left, right):
    return lax.dot_general(left, right, NT, preferred_element_type=F32)


def fold(value, rank):
    return value[:, :rank] + value[:, rank : 2 * rank]


def lanes(value):
    part = value.shape[0] // 2
    return jnp.concatenate([value[:part], value[part:]], axis=1)


def unlanes(values):
    rank = values[0].shape[1] // 2
    above = jnp.concatenate([value[:, :rank] for value in values], axis=1)
    below = jnp.concatenate([value[:, rank:] for value in values], axis=1)
    return jnp.concatenate([above, below], axis=0)


def bring(sources, targets, arrived):
    copies = [
        pltpu.make_async_copy(source, target, arrived.at[n])
        for n, (source, target) in enumerate(zip(sources, targets))
    ]
    for copy in copies:
        copy.start()
    return copies


def coef_kernel(
    x_hbm, basis_hbm, transfer_hbm, parent_hbm, packed_ref, group_ref, own_ref,
    x_ref, basis_ref, transfer_ref, parent_ref, arrived,
):
    leaves, rank, rows = basis_ref.shape
    copies = bring(
        (parent_hbm, x_hbm, basis_hbm, transfer_hbm),
        (parent_ref, x_ref, basis_ref, transfer_ref),
        arrived,
    )
    g = lax.axis_index("leaf")
    copies[0].wait()
    rise = None
    for level in range(Y_BITS):
        step = jnp.where(((g >> level) & 1) == 1, parent_ref[1], parent_ref[0])
        rise = step if rise is None else dot(triple_left(step), triple_right(rise))
    rise = triple_right(rise.T)
    for copy in copies[1:]:
        copy.wait()
    spread, stacked = [], []
    packed_ref[:, : leaves * rows] = x_ref[...]
    for i in range(leaves):
        high, low = halves(dot_nt(x_ref[:, i * rows : (i + 1) * rows], basis_ref[i]))
        both = jnp.concatenate([high, low], axis=1)
        start = leaves * rows + i * 2 * rank
        packed_ref[:, start : start + 2 * rank] = both
        spread.append(both)
    for i in range(leaves):
        above, below = halves(transfer_ref[i])
        twice = jnp.concatenate([above, above], axis=1)
        once = jnp.concatenate([below, jnp.zeros_like(below)], axis=1)
        stacked.append(jnp.concatenate([twice, once], axis=0))
    total = dot_nt(jnp.concatenate(spread, axis=1), jnp.concatenate(stacked, axis=1))
    total = fold(total, rank)
    sent = lanes(dot(triple_left(total), rise).astype(BF16))
    for j in range(group_ref.shape[0]):
        group_ref[j] = sent
    own_ref[...] = lanes(total.astype(BF16))


def path_blocks(g, groups, first, last, down, kind_ref, table_ref, parent_ref, with_sum):
    rank = table_ref.shape[1]
    steps = [triple_left(parent_ref[0]), triple_left(parent_ref[1])]
    across = []
    for level in range(first, last):
        heap = (groups >> (level + 1)) + (g >> (level + 1))
        coupling = table_ref[kind_ref[heap - 1]]
        bit = (g >> level) & 1
        coupling = jnp.where(bit == 1, coupling, coupling.T)
        step = jnp.where(bit == 1, parent_ref[1], parent_ref[0])
        if down is None:
            across.append(coupling)
            down = step
        else:
            right = triple_right(down)
            made = dot(triple_left(jnp.concatenate([coupling, step], axis=0)), right)
            across.append(made[:rank])
            down = made[rank:]
    upward = jnp.concatenate([parent_ref[0].T, parent_ref[1].T], axis=0)
    left = triple_left(upward)
    trees = [[block] for block in across]
    if with_sum:
        trees.append([upward[:rank], upward[rank:]])
    for step in range(1, last - first):
        live = [t for t in range(len(trees)) if t >= step]
        blocks = [block for t in live for block in trees[t]]
        made = dot(left, triple_right(jnp.concatenate(blocks, axis=1)))
        at = 0
        for t in live:
            grown = []
            for _ in trees[t]:
                for b in range(2):
                    grown.append(made[b * rank : (b + 1) * rank, at * rank : (at + 1) * rank])
                at += 1
            trees[t] = grown
    return trees, down


def store_blocks(trees, here, ref, offset):
    rank = ref.shape[1]
    ref[offset + here, :, : 2 * rank] = jnp.zeros((rank, 2 * rank), BF16)
    for t, blocks in enumerate(trees):
        base = ((here >> t) ^ 1) << t
        for v, block in enumerate(blocks):
            ref[offset + base + v, :, : 2 * rank] = jnp.concatenate(halves(block), axis=1)


def path_kernel(
    kind_hbm, table_hbm, parent_hbm, transfer_hbm, z_ref, yx_ref, far_ref, spread_ref,
    kind_ref, table_ref, parent_ref, transfer_ref, arrived,
):
    for copy in bring(
        (kind_hbm, table_hbm, parent_hbm, transfer_hbm),
        (kind_ref, table_ref, parent_ref, transfer_ref),
        arrived,
    ):
        copy.wait()
    g = lax.axis_index("leaf")
    groups = kind_ref.shape[0] + 1
    rank = table_ref.shape[1]
    low, high = Y_BITS, Y_BITS + Z_BITS
    tree = (kind_ref, table_ref, parent_ref)

    trees, inner = path_blocks(g, groups, low, high, None, *tree, True)
    store_blocks(trees[:Z_BITS], (g >> low) & ((1 << Z_BITS) - 1), z_ref, 0)
    for j, block in enumerate(trees[Z_BITS]):
        z_ref[j, :, 2 * rank :] = jnp.concatenate(halves(block), axis=1)

    y_trees, fall = path_blocks(g, groups, 0, low, None, *tree, False)
    both = jnp.concatenate(halves(fall), axis=1)
    for y in range(1 << Y_BITS):
        yx_ref[(1 << (X_BITS + Y_BITS)) + y] = both
    down = dot(triple_left(inner), triple_right(fall))
    x_trees, _ = path_blocks(g, groups, high, high + X_BITS, down, *tree, False)
    here = g >> high
    for t, blocks in enumerate(x_trees):
        base = ((here >> t) ^ 1) << t
        for v, block in enumerate(blocks):
            both = jnp.concatenate(halves(block), axis=1)
            for y in range(1 << Y_BITS):
                yx_ref[((base + v) << Y_BITS) + y] = both
    store_blocks(y_trees, g & ((1 << Y_BITS) - 1), yx_ref, here << Y_BITS)

    for kind in range(table_ref.shape[0]):
        above, below = halves(table_ref[kind])
        far_ref[kind, :rank, :] = jnp.concatenate([above, above], axis=1)
        far_ref[kind, rank:, :] = jnp.concatenate([below, jnp.zeros_like(below)], axis=1)
    for i in range(transfer_ref.shape[0]):
        spread_ref[:, i * rank : (i + 1) * rank] = triple_right(transfer_ref[i])


def middle_kernel(seen_ref, z_ref, own_ref, sent_ref):
    count = seen_ref.shape[0]
    rank = z_ref.shape[1]
    rows = own_ref.shape[0]
    total = dot(
        unlanes([seen_ref[j] for j in range(count)]), z_ref[...].reshape(count * rank, 4 * rank)
    )
    inside = lanes(fold(total[:, : 2 * rank], rank).astype(BF16))
    outside = lanes(fold(total[:, 2 * rank :], rank).astype(BF16))
    own = own_ref[...]
    here = lax.axis_index("leaf") >> (Y_BITS + Z_BITS)
    for x in range(1 << X_BITS):
        mine = here == x
        first, second = jnp.where(mine, own, outside), jnp.where(mine, inside, outside)
        for y in range(1 << Y_BITS):
            sent_ref[(x << Y_BITS) + y, :rows] = first
            sent_ref[(x << Y_BITS) + y, rows:] = second


def near_kernel(
    near_hbm, far_index_hbm, far_kind_hbm,
    before_ref, packed_ref, after_ref, own_ref, other_ref, table_ref,
    out_ref, window, coefs, blocks, arrived,
    near_ref, far_index_ref, far_kind_ref, lists_arrived,
):
    lists = bring(
        (near_hbm, far_index_hbm, far_kind_hbm), (near_ref, far_index_ref, far_kind_ref),
        lists_arrived,
    )
    leaves, slots, half, rows = own_ref.shape
    cols = packed_ref.shape[0]
    rank = coefs.shape[2] // 2
    start = (lax.axis_index("leaf") - 1) * leaves
    core = lax.axis_index("cols")

    def fetch(i, side):
        ref = (own_ref, other_ref)[side]
        row = (core if side == 0 else 1 - core) * half
        to = blocks.at[i, :, pl.ds(pl.multiple_of(row, half), half), :]
        return pltpu.make_async_copy(ref.at[i], to, arrived.at[side, i])

    for i in range(leaves):
        for side in range(2):
            fetch(i, side).start()
    for part, ref in enumerate((before_ref, packed_ref, after_ref)):
        for n in range(leaves):
            window[part * leaves + n] = ref[:, n * rows : (n + 1) * rows]
            at = leaves * rows + n * 2 * rank
            coefs[part * leaves + n] = ref[:, at : at + 2 * rank]
    window[3 * leaves] = jnp.zeros((cols, rows), BF16)
    coefs[3 * leaves] = jnp.zeros((cols, 2 * rank), BF16)
    for copy in lists:
        copy.wait()

    def slot(index):
        return jnp.where(index >= 0, jnp.clip(index - start, 0, 3 * leaves - 1), 3 * leaves)

    def far_leaf(i):
        total = jnp.zeros((cols, 2 * rank), F32)
        for k in range(slots):
            total += dot_nt(coefs[slot(far_index_ref[i, k])], table_ref[far_kind_ref[i, k]])
        return fold(total, rank)

    for i in range(0, leaves, 2):
        at = leaves * rows + i * rank
        out_ref[:, at : at + 2 * rank] = jnp.concatenate([far_leaf(i), far_leaf(i + 1)], axis=1)
    for i in range(leaves):
        if i % 2 == 0:
            for n in (i, i + 1):
                for side in range(2):
                    fetch(n, side).wait()
        total = jnp.zeros((cols, rows), F32)
        for k in range(slots):
            total += dot_nt(window[slot(near_ref[i, k])], blocks[i, k])
        out_ref[:, i * rows : (i + 1) * rows] = total


def last_kernel(seen_ref, yx_ref, spread_ref, local_ref, basis_ref, out_ref):
    count, rows, _ = seen_ref.shape
    leaves, rank, width = basis_ref.shape
    half = rows // 2
    start = (lax.axis_index("leaf") >> (Y_BITS + Z_BITS)) << Y_BITS
    parts = [seen_ref[j, :half] for j in range(count)]
    parts += [seen_ref[start + y, half:] for y in range(1 << Y_BITS)]
    total = dot(unlanes(parts), yx_ref[...].reshape(len(parts) * rank, 2 * rank))
    group = triple_left(fold(total, rank))
    fields = (dot(group, spread_ref[...]) + local_ref[:, leaves * width :]).astype(BF16)
    for i in range(leaves):
        field = fields[:, i * rank : (i + 1) * rank]
        at = slice(i * width, (i + 1) * width)
        out_ref[:, at] = (local_ref[:, at] + dot(field, basis_ref[i])).astype(BF16)


def call(kernel, outs, ins, flops, moved, mib, scratch=()):
    def spec(space):
        return pl.BlockSpec(memory_space=space)

    many = isinstance(outs, tuple)
    return pl.pallas_call(
        kernel,
        out_shape=outs,
        in_specs=[spec(space) for space in ins],
        out_specs=tuple(spec(pltpu.VMEM) for _ in outs) if many else spec(pltpu.VMEM),
        scratch_shapes=list(scratch),
        compiler_params=pltpu.CompilerParams(vmem_limit_bytes=mib << 20),
        cost_estimate=pl.CostEstimate(flops=flops, bytes_accessed=moved, transcendentals=0),
    )


def shards(
    vectors, near_blocks, near_index, far_index, far_kind,
    cluster_basis, leaf_transfer, coupling_table, parent_transfer_matrices, coarse_kind,
):
    cols, width = vectors.shape
    leaves, rank, rows = cluster_basis.shape
    slots = near_index.shape[1]
    kinds = coupling_table.shape[0]
    peers = lax.axis_size("leaf")
    size = 1 << Z_BITS
    across = 1 << (X_BITS + Y_BITS)
    shape = jax.ShapeDtypeStruct
    packed_width = width + leaves * 2 * rank
    vm, hbm = pltpu.VMEM, pltpu.HBM
    kept = lambda space, array: space(array.shape, array.dtype)
    sems = lambda *count: pltpu.SemaphoreType.DMA(count)
    own_line = shape((cols // 2, 2 * rank), BF16)
    line = (1 << Z_BITS) - 1
    z_groups, yx_groups = {}, {}
    for n in range(peers):
        z_groups.setdefault(n & ~(line << Y_BITS), []).append(n)
        yx_groups.setdefault((n >> Y_BITS) & line, []).append(n)
    z_groups, yx_groups = list(z_groups.values()), list(yx_groups.values())
    up = [(n, n + 1) for n in range(peers - 1)]
    stay = lambda *arrays: [pltpu.with_memory_space_constraint(a, hbm) for a in arrays]
    (
        vectors, blocks_here, near_index, far_index, far_kind, basis_here, transfer_here,
        coupling_table, parent_transfer_matrices, coarse_kind,
    ) = stay(
        vectors, near_blocks, near_index, far_index, far_kind, cluster_basis, leaf_transfer,
        coupling_table, parent_transfer_matrices, coarse_kind,
    )

    packed, group, own = call(
        coef_kernel,
        (
            shape((cols, packed_width), BF16),
            shape((size, *own_line.shape), BF16),
            own_line,
        ),
        [hbm] * 4, 2**26, 2**20, 4,
        [
            kept(vm, vectors), kept(vm, cluster_basis), kept(vm, leaf_transfer),
            kept(vm, parent_transfer_matrices), sems(4),
        ],
    )(vectors, basis_here, transfer_here, parent_transfer_matrices)
    seen_z = lax.all_to_all(group, "leaf", 0, 0, axis_index_groups=z_groups, tiled=True)
    before = lax.ppermute(packed, "leaf", up)
    after = lax.ppermute(packed, "leaf", [(b, a) for a, b in up])
    other_blocks = lax.ppermute(near_blocks, "cols", [(0, 1), (1, 0)])
    z_table, yx_table, far_table, spread = call(
        path_kernel,
        (
            shape((size, rank, 4 * rank), BF16),
            shape((across + (1 << Y_BITS), rank, 2 * rank), BF16),
            shape((kinds, 2 * rank, 2 * rank), BF16),
            shape((3 * rank, leaves * rank), BF16),
        ),
        [hbm] * 4, 2**28, 2**20, 8,
        [
            kept(pltpu.SMEM, coarse_kind), kept(vm, coupling_table),
            kept(vm, parent_transfer_matrices), kept(vm, leaf_transfer), sems(4),
        ],
    )(coarse_kind, coupling_table, parent_transfer_matrices, transfer_here)
    sent = call(
        middle_kernel, shape((across, cols, 2 * rank), BF16),
        [vm] * 3, 2**25, 2**19, 4,
    )(seen_z, z_table, own)
    seen_yx = lax.all_to_all(sent, "leaf", 0, 0, axis_index_groups=yx_groups, tiled=True)
    local = call(
        near_kernel,
        shape((cols, width + leaves * rank), F32),
        [hbm] * 3 + [vm] * 3 + [hbm] * 2 + [vm], 2**30, 10 * 2**20, 16,
        [
            pltpu.VMEM((3 * leaves + 1, cols, rows), BF16),
            pltpu.VMEM((3 * leaves + 1, cols, 2 * rank), BF16),
            pltpu.VMEM((leaves, slots, rows, rows), BF16),
            sems(2, leaves),
            kept(pltpu.SMEM, near_index), kept(pltpu.SMEM, far_index),
            kept(pltpu.SMEM, far_kind), sems(3),
        ],
    )(
        near_index, far_index, far_kind,
        before, packed, after, blocks_here, stay(other_blocks)[0], far_table,
    )
    return call(
        last_kernel, shape((cols, width), BF16), [vm] * 5, 2**27, 2**21, 8
    )(seen_yx, yx_table, spread, local, cluster_basis)


def solution(mesh):
    in_specs = (
        P("cols", "leaf"),
        P("leaf", None, "cols", None),
        P("leaf", None),
        P("leaf", None),
        P("leaf", None),
        P("leaf", None, None),
        P("leaf", None, None),
        P(),
        P(),
        P(),
    )
    out_specs = P("cols", "leaf")
    return jax.shard_map(shards, mesh=mesh, in_specs=in_specs, out_specs=out_specs, check_vma=False)
```
